512 devices in a mesh: iface: 512 (over y, z, x, core).
Axes of the slice: x: 4, y: 8, z: 8, core: 2. Of those that a mesh axis runs over, the one named last changes fastest.
Arguments:
- res_diffs: float32 [128, 2, 1048576], P(None, None, 'iface'), may hold values from -400 to 400, as said below
- out_diffs: float32 [128, 2, 1048576], P(None, None, 'iface'), may hold values from -0.5 to 0.5
- residual: float32 [2, 1048576], P(None, 'iface'), may hold values from -60000 to 60000
Outputs:
- correction: float32 [2, 1048576], P(None, 'iface')
- coefficients: float32 [128], replicated
The draws below stay inside these ranges and needn't reach their ends.
Inputs may be any that keep to these rules, and one draw needn't show every extreme that they name: `res_diffs`: columns are linearly independent.
All inputs are finite; a program needn't handle non-finite values.
Results may differ from the reference program's by a relative error of at most 0.00016.
Values sent between devices are 32-bit elements; how exact they have to be, the bound alone decides.
No kernel may reach another device: no remote copies, remote signals or barrier semaphores. Data moves between devices by JAX's collectives and lax.ppermute only.
A program may use at most 64 MiB of HBM per device.

```python
import jax
import jax.numpy as jnp
from jax import lax

M = 128
F = 2
ROWS = 1048576


def shared_fields(key):
    key = jax.random.fold_in(key, 4711)
    keys = jax.random.split(key, 5)
    col_scale = jnp.exp(jax.random.uniform(keys[0], (M,), jnp.float32, jnp.log(0.5), jnp.log(2.0)))
    position = jnp.arange(ROWS).astype(jnp.float32) / ROWS
    row_scale = jnp.exp(jax.random.uniform(keys[1], (ROWS,), jnp.float32, 0.0, jnp.log(10.0))) * (1.0 + 2.0 * position)
    base = jax.random.normal(keys[2], (M, F, ROWS), jnp.float32)
    field_scale = 6.0 ** (jnp.arange(F).astype(jnp.float32) / (F - 1))
    reach = 6.0
    columns = base * col_scale[:, None, None] * row_scale[None, None, :]
    mixing = jax.random.normal(keys[3], (M,), jnp.float32)
    noise = jax.random.normal(keys[4], (F, ROWS), jnp.float32) * row_scale[None, :]
    fitted = jnp.einsum('m,mfi->fi', mixing, columns) / jnp.sqrt(1.0 * M)
    share = jnp.arange(F).astype(jnp.float32)[:, None] / (F - 1)
    slope = (1.0 - share) * position[None, :] + share * (1.0 - position[None, :])
    profile = 1.0 + (reach - 1.0) * slope
    resid = field_scale[:, None] * profile * (fitted + 0.7 * noise)
    return (columns, resid)


def draw_res_diffs(key, part):
    return shared_fields(key)[0]


def draw_residual(key, part):
    return shared_fields(key)[1]


def shard_levels(stream_key, shape, shards, smallest, high):
    gain = 1.0
    for axis_at, shards_of in shards:
        steps = jax.random.uniform(jax.random.fold_in(jax.random.fold_in(stream_key, 6), axis_at), (shards_of,), jnp.float32, smallest / len(shards), high / len(shards))
        gain = gain * jnp.repeat(jnp.exp(steps), shape[axis_at] // shards_of).reshape((-1,) + (1,) * (len(shape) - 1 - axis_at))
    return gain


def centred(rng, dims, width, bound, pieces=(), dtype=jnp.bfloat16):
    entries = width * jax.random.normal(rng, dims, jnp.float32)
    if pieces:
        entries = entries * shard_levels(rng, dims, pieces, -0.22, 0.18)
    return jnp.clip(entries, -bound, bound).astype(dtype)


def setup_inputs(seed: int = 0) -> dict:
    seeds = jax.random.split(jax.random.key(seed), 4)
    return {
        "res_diffs": draw_res_diffs(jax.random.fold_in(seeds[3], 71), 0),
        "out_diffs": centred(seeds[1], (M, F, ROWS), M ** -0.5, 0.5, ((2, 512),), jnp.float32),
        "residual": draw_residual(jax.random.fold_in(seeds[3], 71), 0),
    }


def reference(res_diffs, out_diffs, residual):
    precise = lax.Precision.HIGHEST
    squares = lax.optimization_barrier(jnp.sum(residual * residual, axis=1))
    weights = lax.rsqrt(squares / ROWS + 1e-06)
    scaled = (res_diffs * weights[None, :, None]).reshape(M, -1)
    target = (residual * weights[:, None]).reshape(-1)
    gram = jnp.dot(scaled.astype(jnp.float32), scaled.T.astype(jnp.float32), precision=precise, preferred_element_type=jnp.float32)
    proj = jnp.dot(scaled.astype(jnp.float32), target.astype(jnp.float32), precision=precise, preferred_element_type=jnp.float32)
    coefficients = jnp.linalg.solve(gram, -proj)
    correction = jnp.dot(coefficients.astype(jnp.float32), out_diffs.reshape(M, -1).astype(jnp.float32), precision=precise, preferred_element_type=jnp.float32)
    return (correction.reshape(F, ROWS), coefficients)
```

```python
import jax
import jax.numpy as jnp
from jax import lax
from jax.experimental import pallas as pl
from jax.experimental.pallas import tpu as pltpu
from jax.sharding import PartitionSpec as P

AXIS = "iface"
LANES = 128
EPSILON = 1e-06
TOLERANCE = 1e-06
STEPS_MAX = 16
INNER = ("y0", "x1", "x0", "c")
BITS = ("y2", "y1", "y0", "z2", "z1", "z0", "x1", "x0", "c")


def groups_over(names):
    count = len(BITS)
    found = {}
    for device in range(1 << count):
        bits = [(device >> (count - 1 - k)) & 1 for k in range(count)]
        key = tuple(b for b, name in zip(bits, BITS) if name not in names)
        found.setdefault(key, []).append(device)
    return list(found.values())


def rows_of(x):
    lead = x.shape[:-2]
    fields, n = x.shape[-2:]
    blocks = x.reshape(lead + (fields, n // LANES, LANES))
    return jnp.swapaxes(blocks, -3, -2).reshape(lead + (fields * n // LANES, LANES))


def eye_mask(m):
    return lax.broadcasted_iota(jnp.int32, (m, m), 0) == lax.broadcasted_iota(jnp.int32, (m, m), 1)


def as_row(column, eye):
    return jnp.sum(jnp.where(eye, column, 0.0), axis=0, keepdims=True)


def as_column(row, eye):
    m = eye.shape[0]
    return jnp.broadcast_to(jnp.sum(jnp.where(eye, row, 0.0), axis=1, keepdims=True), (m, m))


def gram_kernel(diffs_ref, residual_ref, out_ref, staged, parts, sems):
    m = diffs_ref.shape[0]
    rows = diffs_ref.shape[1]
    order = [*range(0, rows, 2), *range(1, rows, 2)]
    copies = {}
    for j in order:
        copies[j] = pltpu.make_async_copy(diffs_ref.at[:, j, :], staged.at[j], sems.at[j])
        copies[j].start()
    eye = eye_mask(m)
    residual = residual_ref[...]
    parity = lax.broadcasted_iota(jnp.int32, residual.shape, 0) & 1
    grams, projs, squares = [], [], []
    for f in range(2):
        proj = None
        for k in range(rows // 2):
            j = 2 * k + f
            copies[j].wait()
            block = staged[j]
            term = block * residual_ref[j : j + 1, :]
            proj = term if proj is None else proj + term
            high = block.astype(jnp.bfloat16)
            rest = block - high.astype(jnp.float32)
            middle = rest.astype(jnp.bfloat16)
            low = (rest - middle.astype(jnp.float32)).astype(jnp.bfloat16)
            columns = slice(k * LANES, (k + 1) * LANES)
            parts[f, 0:m, columns] = high
            parts[f, m : 2 * m, columns] = middle
            parts[f, 2 * m : 3 * m, columns] = low
        product = lax.dot_general(
            parts[f], parts[f, 0 : 2 * m, :], (((1,), (1,)), ((), ())), preferred_element_type=jnp.float32
        )
        cross = product[2 * m : 3 * m, 0:m]
        gram = (product[m : 2 * m, m : 2 * m] + (cross + cross.T)) + (
            product[0:m, m : 2 * m] + product[m : 2 * m, 0:m]
        )
        grams.append(gram + product[0:m, 0:m])
        projs.append(as_row(jnp.sum(proj, axis=1, keepdims=True), eye))
        own = jnp.where(parity == f, residual * residual, 0.0)
        total = jnp.sum(jnp.sum(own, axis=0, keepdims=True), axis=1, keepdims=True)
        squares.append(jnp.broadcast_to(total, (1, LANES)))
    below = lax.broadcasted_iota(jnp.int32, (m, m), 0) > lax.broadcasted_iota(jnp.int32, (m, m), 1)
    out_ref[0:m, :] = jnp.where(below, grams[0], grams[1])
    diagonal = jnp.sum(jnp.where(eye, grams[0], 0.0), axis=0, keepdims=True)
    at = lax.broadcasted_iota(jnp.int32, (out_ref.shape[0] - m, LANES), 0)
    extra = jnp.zeros(at.shape, jnp.float32)
    for i, row in enumerate((projs[0], projs[1], diagonal, squares[0], squares[1])):
        extra = jnp.where(at == i, row, extra)
    out_ref[m:, :] = extra


def solve_kernel(rows_all, sums_ref, diffs_ref, correction_ref, coefficients_ref, staged, matrix, x, r, p, sem):
    m = diffs_ref.shape[0]
    copy = pltpu.make_async_copy(diffs_ref, staged, sem)
    copy.start()
    eye = eye_mask(m)
    below = lax.broadcasted_iota(jnp.int32, (m, m), 0) > lax.broadcasted_iota(jnp.int32, (m, m), 1)
    packed = sums_ref[0:m, :]
    extra = sums_ref[m : m + 8, :]
    w0 = 1.0 / (extra[3:4, :] / rows_all + EPSILON)
    w1 = 1.0 / (extra[4:5, :] / rows_all + EPSILON)
    turned = packed.T
    gram = jnp.where(below, w0 * packed + w1 * turned, w1 * packed + w0 * turned)
    gram = jnp.where(eye, w1 * packed + w0 * extra[2:3, :], gram)
    b_row = -(w0 * extra[0:1, :] + w1 * extra[1:2, :])
    only = jnp.where(eye, gram, 0.0)
    scale_row = lax.rsqrt(jnp.sum(only, axis=0, keepdims=True))
    scale = lax.rsqrt(jnp.broadcast_to(jnp.sum(only, axis=1, keepdims=True), (m, m)))
    matrix[...] = (scale * gram) * scale_row
    b = as_column(b_row * scale_row, eye)
    x[...] = jnp.zeros((m, m), jnp.float32)
    r[...] = b
    p[...] = b

    def dot(u, v):
        return jnp.sum(u * v, axis=0, keepdims=True)

    def ratio(top, bottom):
        return jnp.where(bottom > 0.0, top / jnp.where(bottom > 0.0, bottom, 1.0), 0.0)

    start = dot(b, b)
    limit = start[0, 0] * (TOLERANCE * TOLERANCE)

    def going(state):
        step, size, _ = state
        return (step < STEPS_MAX) & (size > limit)

    def advance(state):
        step, _, rr = state
        direction = p[...]
        image = jnp.broadcast_to(
            jnp.sum(matrix[...] * as_row(direction, eye), axis=1, keepdims=True), (m, m)
        )
        alpha = ratio(rr, dot(direction, image))
        x[...] += alpha * direction
        rest = r[...] - alpha * image
        r[...] = rest
        after = dot(rest, rest)
        p[...] = rest + ratio(after, rr) * direction
        return step + 1, after[0, 0], after

    _, size, _ = lax.while_loop(going, advance, (0, start[0, 0], start))

    @pl.when(size > limit)
    def _():
        r[...] = b

        @pl.loop(0, m)
        def _(k):
            lane = lax.broadcasted_iota(jnp.int32, (m, m), 1)
            line = lax.broadcasted_iota(jnp.int32, (m, m), 0)
            here = matrix[...]
            row = matrix[pl.ds(k, 1), :]
            value = r[pl.ds(k, 1), :]
            column = jnp.sum(jnp.where(lane == k, here, 0.0), axis=1, keepdims=True)
            pivot = jnp.sum(jnp.where(lane[0:1] == k, row, 0.0), axis=1, keepdims=True)
            factor = jnp.where(line == k, 0.0, column / pivot)
            matrix[...] = here - factor * row
            r[...] = r[...] - factor * value

        x[...] = r[...] / jnp.broadcast_to(
            jnp.sum(jnp.where(eye, matrix[...], 0.0), axis=1, keepdims=True), (m, m)
        )

    found = scale * x[...]
    x[...] = found
    coefficients_ref[...] = as_row(found, eye)
    copy.wait()
    lines = correction_ref.shape[0]
    totals = [jnp.zeros((lines, LANES), jnp.float32) for _ in range(2)]
    for k in range(m):
        totals[k % 2] += staged[k] * x[k : k + 1, :]
    correction_ref[...] = totals[0] + totals[1]


def local_sums(res_diffs, residual, lines):
    m = res_diffs.shape[0]
    diffs = rows_of(res_diffs)
    rows = diffs.shape[1]
    return pl.pallas_call(
        gram_kernel,
        out_shape=jax.ShapeDtypeStruct((lines, LANES), jnp.float32),
        in_specs=[pl.BlockSpec(memory_space=pl.ANY), pl.BlockSpec(memory_space=pltpu.VMEM)],
        out_specs=pl.BlockSpec(memory_space=pltpu.VMEM),
        scratch_shapes=[
            pltpu.VMEM((rows, m, LANES), jnp.float32),
            pltpu.VMEM((2, 3 * m, rows // 2 * LANES), jnp.bfloat16),
            pltpu.SemaphoreType.DMA((rows,)),
        ],
        name="gram",
    )(diffs, rows_of(residual))


def solve_and_apply(sums, out_diffs, rows_all):
    m = out_diffs.shape[0]
    diffs = rows_of(out_diffs)
    lines = diffs.shape[1]
    square = pltpu.VMEM((m, LANES), jnp.float32)
    correction, coefficients = pl.pallas_call(
        lambda *refs: solve_kernel(rows_all, *refs),
        out_shape=(
            jax.ShapeDtypeStruct((lines, LANES), jnp.float32),
            jax.ShapeDtypeStruct((1, m), jnp.float32),
        ),
        in_specs=[pl.BlockSpec(memory_space=pltpu.VMEM), pl.BlockSpec(memory_space=pl.ANY)],
        out_specs=(pl.BlockSpec(memory_space=pltpu.VMEM), pl.BlockSpec(memory_space=pltpu.VMEM)),
        scratch_shapes=[pltpu.VMEM((m, lines, LANES), jnp.float32), square, square, square, square, pltpu.SemaphoreType.DMA],
        name="solve",
    )(sums, diffs)
    fields = out_diffs.shape[1]
    blocks = correction.reshape(lines // fields, fields, LANES)
    return jnp.swapaxes(blocks, 0, 1).reshape(fields, -1), coefficients.reshape(m)


def exchange(chunks, groups):
    return lax.all_to_all(chunks, AXIS, 0, 0, axis_index_groups=groups)


def on_device(res_diffs, out_diffs, residual):
    rows_all = residual.shape[1] * lax.axis_size(AXIS)
    inner = groups_over(INNER)
    outer = groups_over([name for name in BITS if name not in INNER])
    pieces = len(inner[0])
    lines = -(-133 // pieces) * pieces
    sums = local_sums(res_diffs, residual, lines)
    part = jnp.sum(exchange(sums.reshape(pieces, 1, -1), inner), axis=0)
    part = jnp.sum(exchange(jnp.broadcast_to(part, (len(outer[0]),) + part.shape), outer), axis=0)
    whole = exchange(jnp.broadcast_to(part, (pieces,) + part.shape), inner)
    return solve_and_apply(whole.reshape(lines, LANES), out_diffs, rows_all)


def solution(mesh):
    placed = (P(None, None, AXIS), P(None, None, AXIS), P(None, AXIS))
    return jax.shard_map(
        on_device, mesh=mesh, in_specs=placed, out_specs=(P(None, AXIS), P()), check_vma=False
    )
```

```python
import jax
import jax.numpy as jnp
from jax import lax
from jax.experimental import pallas as pl
from jax.experimental.pallas import tpu as pltpu
from jax.sharding import PartitionSpec as P

AXIS = "iface"
LANES = 128
EPSILON = 1e-06
TOLERANCE = 1e-06
STEPS_MAX = 16
INNER = ("y0", "z0", "x1", "x0", "c")
BITS = ("y2", "y1", "y0", "z2", "z1", "z0", "x1", "x0", "c")


def groups_over(names):
    count = len(BITS)
    found = {}
    for device in range(1 << count):
        bits = [(device >> (count - 1 - k)) & 1 for k in range(count)]
        key = tuple(b for b, name in zip(bits, BITS) if name not in names)
        found.setdefault(key, []).append(device)
    return list(found.values())


def rows_of(x):
    lead = x.shape[:-2]
    fields, n = x.shape[-2:]
    blocks = x.reshape(lead + (fields, n // LANES, LANES))
    return jnp.swapaxes(blocks, -3, -2).reshape(lead + (fields * n // LANES, LANES))


def eye_mask(m):
    return lax.broadcasted_iota(jnp.int32, (m, m), 0) == lax.broadcasted_iota(jnp.int32, (m, m), 1)


def as_row(column, eye):
    return jnp.sum(jnp.where(eye, column, 0.0), axis=0, keepdims=True)


def as_column(row, eye):
    m = eye.shape[0]
    return jnp.broadcast_to(jnp.sum(jnp.where(eye, row, 0.0), axis=1, keepdims=True), (m, m))


def gram_kernel(diffs_ref, residual_ref, out_ref, staged, parts, sems):
    m = diffs_ref.shape[0]
    rows = diffs_ref.shape[1]
    order = [*range(0, rows, 2), *range(1, rows, 2)]
    copies = {}
    for j in order:
        copies[j] = pltpu.make_async_copy(diffs_ref.at[:, j, :], staged.at[j], sems.at[j])
        copies[j].start()
    eye = eye_mask(m)
    residual = residual_ref[...]
    parity = lax.broadcasted_iota(jnp.int32, residual.shape, 0) & 1
    grams, projs, squares = [], [], []
    for f in range(2):
        proj = None
        for k in range(rows // 2):
            j = 2 * k + f
            copies[j].wait()
            block = staged[j]
            term = block * residual_ref[j : j + 1, :]
            proj = term if proj is None else proj + term
            high = block.astype(jnp.bfloat16)
            rest = block - high.astype(jnp.float32)
            middle = rest.astype(jnp.bfloat16)
            low = (rest - middle.astype(jnp.float32)).astype(jnp.bfloat16)
            columns = slice(k * LANES, (k + 1) * LANES)
            parts[f, 0:m, columns] = high
            parts[f, m : 2 * m, columns] = middle
            parts[f, 2 * m : 3 * m, columns] = low
        product = lax.dot_general(
            parts[f], parts[f, 0 : 2 * m, :], (((1,), (1,)), ((), ())), preferred_element_type=jnp.float32
        )
        cross = product[2 * m : 3 * m, 0:m]
        gram = (product[m : 2 * m, m : 2 * m] + (cross + cross.T)) + (
            product[0:m, m : 2 * m] + product[m : 2 * m, 0:m]
        )
        grams.append(gram + product[0:m, 0:m])
        projs.append(as_row(jnp.sum(proj, axis=1, keepdims=True), eye))
        own = jnp.where(parity == f, residual * residual, 0.0)
        total = jnp.sum(jnp.sum(own, axis=0, keepdims=True), axis=1, keepdims=True)
        squares.append(jnp.broadcast_to(total, (1, LANES)))
    below = lax.broadcasted_iota(jnp.int32, (m, m), 0) > lax.broadcasted_iota(jnp.int32, (m, m), 1)
    out_ref[0:m, :] = jnp.where(below, grams[0], grams[1])
    diagonal = jnp.sum(jnp.where(eye, grams[0], 0.0), axis=0, keepdims=True)
    at = lax.broadcasted_iota(jnp.int32, (out_ref.shape[0] - m, LANES), 0)
    extra = jnp.zeros(at.shape, jnp.float32)
    for i, row in enumerate((projs[0], projs[1], diagonal, squares[0], squares[1])):
        extra = jnp.where(at == i, row, extra)
    out_ref[m:, :] = extra


def solve_kernel(rows_all, sums_ref, diffs_ref, correction_ref, coefficients_ref, staged, matrix, x, r, p, sem):
    m = diffs_ref.shape[0]
    copy = pltpu.make_async_copy(diffs_ref, staged, sem)
    copy.start()
    eye = eye_mask(m)
    below = lax.broadcasted_iota(jnp.int32, (m, m), 0) > lax.broadcasted_iota(jnp.int32, (m, m), 1)
    packed = sums_ref[0:m, :]
    extra = sums_ref[m : m + 8, :]
    w0 = 1.0 / (extra[3:4, :] / rows_all + EPSILON)
    w1 = 1.0 / (extra[4:5, :] / rows_all + EPSILON)
    turned = packed.T
    gram = jnp.where(below, w0 * packed + w1 * turned, w1 * packed + w0 * turned)
    gram = jnp.where(eye, w1 * packed + w0 * extra[2:3, :], gram)
    b_row = -(w0 * extra[0:1, :] + w1 * extra[1:2, :])
    only = jnp.where(eye, gram, 0.0)
    scale_row = lax.rsqrt(jnp.sum(only, axis=0, keepdims=True))
    scale = lax.rsqrt(jnp.broadcast_to(jnp.sum(only, axis=1, keepdims=True), (m, m)))
    matrix[...] = (scale * gram) * scale_row
    b = as_column(b_row * scale_row, eye)
    x[...] = jnp.zeros((m, m), jnp.float32)
    r[...] = b
    p[...] = b

    def dot(u, v):
        return jnp.sum(u * v, axis=0, keepdims=True)

    def ratio(top, bottom):
        return jnp.where(bottom > 0.0, top / jnp.where(bottom > 0.0, bottom, 1.0), 0.0)

    start = dot(b, b)
    limit = start[0, 0] * (TOLERANCE * TOLERANCE)

    def going(state):
        step, size, _ = state
        return (step < STEPS_MAX) & (size > limit)

    def advance(state):
        step, _, rr = state
        direction = p[...]
        image = jnp.broadcast_to(
            jnp.sum(matrix[...] * as_row(direction, eye), axis=1, keepdims=True), (m, m)
        )
        alpha = ratio(rr, dot(direction, image))
        x[...] += alpha * direction
        rest = r[...] - alpha * image
        r[...] = rest
        after = dot(rest, rest)
        p[...] = rest + ratio(after, rr) * direction
        return step + 1, after[0, 0], after

    _, size, _ = lax.while_loop(going, advance, (0, start[0, 0], start))

    @pl.when(size > limit)
    def _():
        r[...] = b

        @pl.loop(0, m)
        def _(k):
            lane = lax.broadcasted_iota(jnp.int32, (m, m), 1)
            line = lax.broadcasted_iota(jnp.int32, (m, m), 0)
            here = matrix[...]
            row = matrix[pl.ds(k, 1), :]
            value = r[pl.ds(k, 1), :]
            column = jnp.sum(jnp.where(lane == k, here, 0.0), axis=1, keepdims=True)
            pivot = jnp.sum(jnp.where(lane[0:1] == k, row, 0.0), axis=1, keepdims=True)
            factor = jnp.where(line == k, 0.0, column / pivot)
            matrix[...] = here - factor * row
            r[...] = r[...] - factor * value

        x[...] = r[...] / jnp.broadcast_to(
            jnp.sum(jnp.where(eye, matrix[...], 0.0), axis=1, keepdims=True), (m, m)
        )

    found = scale * x[...]
    x[...] = found
    coefficients_ref[...] = as_row(found, eye)
    copy.wait()
    lines = correction_ref.shape[0]
    totals = [jnp.zeros((lines, LANES), jnp.float32) for _ in range(2)]
    for k in range(m):
        totals[k % 2] += staged[k] * x[k : k + 1, :]
    correction_ref[...] = totals[0] + totals[1]


def local_sums(res_diffs, residual, lines):
    m = res_diffs.shape[0]
    diffs = rows_of(res_diffs)
    rows = diffs.shape[1]
    return pl.pallas_call(
        gram_kernel,
        out_shape=pltpu.VMEM((lines, LANES), jnp.float32),
        in_specs=[pl.BlockSpec(memory_space=pl.ANY), pl.BlockSpec(memory_space=pltpu.VMEM)],
        out_specs=pl.BlockSpec(memory_space=pltpu.VMEM),
        scratch_shapes=[
            pltpu.VMEM((rows, m, LANES), jnp.float32),
            pltpu.VMEM((2, 3 * m, rows // 2 * LANES), jnp.bfloat16),
            pltpu.SemaphoreType.DMA((rows,)),
        ],
        name="gram",
    )(diffs, rows_of(residual))


def solve_and_apply(sums, out_diffs, rows_all):
    m = out_diffs.shape[0]
    diffs = rows_of(out_diffs)
    lines = diffs.shape[1]
    square = pltpu.VMEM((m, LANES), jnp.float32)
    correction, coefficients = pl.pallas_call(
        lambda *refs: solve_kernel(rows_all, *refs),
        out_shape=(
            jax.ShapeDtypeStruct((lines, LANES), jnp.float32),
            jax.ShapeDtypeStruct((1, m), jnp.float32),
        ),
        in_specs=[pl.BlockSpec(memory_space=pltpu.VMEM), pl.BlockSpec(memory_space=pl.ANY)],
        out_specs=(pl.BlockSpec(memory_space=pltpu.VMEM), pl.BlockSpec(memory_space=pltpu.VMEM)),
        scratch_shapes=[pltpu.VMEM((m, lines, LANES), jnp.float32), square, square, square, square, pltpu.SemaphoreType.DMA],
        name="solve",
    )(pltpu.with_memory_space_constraint(sums, pltpu.VMEM), diffs)
    fields = out_diffs.shape[1]
    blocks = correction.reshape(lines // fields, fields, LANES)
    return jnp.swapaxes(blocks, 0, 1).reshape(fields, -1), coefficients.reshape(m)


def exchange(chunks, groups):
    return lax.all_to_all(chunks, AXIS, 0, 0, axis_index_groups=groups)


def on_device(res_diffs, out_diffs, residual):
    rows_all = residual.shape[1] * lax.axis_size(AXIS)
    inner = groups_over(INNER)
    outer = groups_over([name for name in BITS if name not in INNER])
    pieces = len(inner[0])
    lines = -(-133 // pieces) * pieces
    sums = local_sums(res_diffs, residual, lines)
    part = jnp.sum(exchange(sums.reshape(pieces, 1, -1), inner), axis=0)
    part = jnp.sum(exchange(jnp.broadcast_to(part, (len(outer[0]),) + part.shape), outer), axis=0)
    whole = exchange(jnp.broadcast_to(part, (pieces,) + part.shape), inner)
    return solve_and_apply(whole.reshape(lines, LANES), out_diffs, rows_all)


def solution(mesh):
    placed = (P(None, None, AXIS), P(None, None, AXIS), P(None, AXIS))
    return jax.shard_map(
        on_device, mesh=mesh, in_specs=placed, out_specs=(P(None, AXIS), P()), check_vma=False
    )
```

```python
import jax
import jax.numpy as jnp
from jax import lax
from jax.experimental import pallas as pl
from jax.experimental.pallas import tpu as pltpu
from jax.sharding import PartitionSpec as P

AXIS = "iface"
LANES = 128
SUBLANES = 8
EPSILON = 1e-06
TOLERANCE = 1e-06
STEPS_MAX = 16
INNER = ('y0', 'x1', 'x0', 'c')
STEPS = [('y2', 'y1', 'z2', 'z1', 'z0')]
BITS = ("y2", "y1", "y0", "z2", "z1", "z0", "x1", "x0", "c")


def groups_over(names):
    count = len(BITS)
    found = {}
    for device in range(1 << count):
        bits = [(device >> (count - 1 - k)) & 1 for k in range(count)]
        key = tuple(b for b, name in zip(bits, BITS) if name not in names)
        found.setdefault(key, []).append(device)
    return list(found.values())


def rows_of(x):
    lead = x.shape[:-2]
    fields, n = x.shape[-2:]
    blocks = x.reshape(lead + (fields, n // LANES, LANES))
    return jnp.swapaxes(blocks, -3, -2).reshape(lead + (fields * n // LANES, LANES))


def eye_mask(m):
    return lax.broadcasted_iota(jnp.int32, (m, m), 0) == lax.broadcasted_iota(jnp.int32, (m, m), 1)


def as_row(column, eye):
    return jnp.sum(jnp.where(eye, column, 0.0), axis=0, keepdims=True)


def as_column(row, eye):
    m = eye.shape[0]
    return jnp.broadcast_to(jnp.sum(jnp.where(eye, row, 0.0), axis=1, keepdims=True), (m, m))


def split(x):
    high = x.astype(jnp.bfloat16)
    rest = x - high.astype(jnp.float32)
    middle = rest.astype(jnp.bfloat16)
    return high, middle, (rest - middle.astype(jnp.float32)).astype(jnp.bfloat16)


def gram_kernel(diffs_ref, residual_ref, out_ref, staged, sems):
    m, rows = diffs_ref.shape[:2]
    tiles = rows // SUBLANES
    copies = [
        pltpu.make_async_copy(
            diffs_ref.at[:, t * SUBLANES : (t + 1) * SUBLANES, :], staged.at[t], sems.at[t]
        )
        for t in range(tiles)
    ]
    for copy in copies:
        copy.start()
    eye = eye_mask(m)
    residual = residual_ref[...]
    parity = lax.broadcasted_iota(jnp.int32, residual.shape, 0) & 1
    squares = []
    for f in range(2):
        own = jnp.where(parity == f, residual * residual, 0.0)
        total = jnp.sum(jnp.sum(own, axis=0, keepdims=True), axis=1, keepdims=True)
        squares.append(jnp.broadcast_to(total, (1, LANES)))
    projs = [jnp.zeros((m, LANES), jnp.float32)] * 2
    products = [jnp.zeros((3 * m, 2 * m), jnp.float32)] * 2
    for t in range(tiles):
        copies[t].wait()
        lines = staged.at[t].reshape(m * SUBLANES, LANES)
        for f in range(2):
            parts = []
            for s in range(f, SUBLANES, 2):
                block = lines[pl.ds(s, m, stride=SUBLANES), :]
                row = t * SUBLANES + s
                projs[f] = projs[f] + block * residual_ref[row : row + 1, :]
                parts.append(split(block))
            high, middle, low = (jnp.concatenate(part, axis=1) for part in zip(*parts))
            products[f] = products[f] + lax.dot_general(
                jnp.concatenate([high, middle, low], axis=0),
                jnp.concatenate([high, middle], axis=0),
                (((1,), (1,)), ((), ())),
                preferred_element_type=jnp.float32,
            )
    grams = []
    for product in products:
        cross = product[2 * m :, 0:m]
        small = product[m : 2 * m, m:] + (cross + cross.T)
        grams.append(product[0:m, 0:m] + (small + (product[0:m, m:] + product[m : 2 * m, 0:m])))
    below = lax.broadcasted_iota(jnp.int32, (m, m), 0) > lax.broadcasted_iota(jnp.int32, (m, m), 1)
    out_ref[0:m, :] = jnp.where(below, grams[0], grams[1])
    lines = [as_row(jnp.sum(proj, axis=1, keepdims=True), eye) for proj in projs]
    lines += [as_row(grams[0], eye), *squares]
    at = lax.broadcasted_iota(jnp.int32, (out_ref.shape[0] - m, LANES), 0)
    extra = jnp.zeros(at.shape, jnp.float32)
    for i, line in enumerate(lines):
        extra = jnp.where(at == i, line, extra)
    out_ref[m:, :] = extra


def solve_kernel(rows_all, sums_ref, diffs_ref, correction_ref, coefficients_ref, matrix, x, r, p):
    m = diffs_ref.shape[0]
    eye = eye_mask(m)
    below = lax.broadcasted_iota(jnp.int32, (m, m), 0) > lax.broadcasted_iota(jnp.int32, (m, m), 1)
    packed = sums_ref[0:m, :]
    extra = sums_ref[m : m + 8, :]
    w0 = 1.0 / (extra[3:4, :] / rows_all + EPSILON)
    w1 = 1.0 / (extra[4:5, :] / rows_all + EPSILON)
    turned = packed.T
    gram = jnp.where(below, w0 * packed + w1 * turned, w1 * packed + w0 * turned)
    gram = jnp.where(eye, w1 * packed + w0 * extra[2:3, :], gram)
    b_row = -(w0 * extra[0:1, :] + w1 * extra[1:2, :])
    only = jnp.where(eye, gram, 0.0)
    scale_row = lax.rsqrt(jnp.sum(only, axis=0, keepdims=True))
    scale = lax.rsqrt(jnp.broadcast_to(jnp.sum(only, axis=1, keepdims=True), (m, m)))
    matrix[...] = (scale * gram) * scale_row
    b = as_column(b_row * scale_row, eye)
    x[...] = jnp.zeros((m, m), jnp.float32)
    r[...] = b
    p[...] = b

    def dot(u, v):
        return jnp.sum(u * v, axis=0, keepdims=True)

    def ratio(top, bottom):
        return jnp.where(bottom > 0.0, top / jnp.where(bottom > 0.0, bottom, 1.0), 0.0)

    start = dot(b, b)
    limit = start[0, 0] * (TOLERANCE * TOLERANCE)

    def going(state):
        step, size, _ = state
        return (step < STEPS_MAX) & (size > limit)

    def advance(state):
        step, _, rr = state
        direction = p[...]
        image = jnp.broadcast_to(
            jnp.sum(matrix[...] * as_row(direction, eye), axis=1, keepdims=True), (m, m)
        )
        alpha = ratio(rr, dot(direction, image))
        x[...] += alpha * direction
        rest = r[...] - alpha * image
        r[...] = rest
        after = dot(rest, rest)
        p[...] = rest + ratio(after, rr) * direction
        return step + 1, after[0, 0], after

    _, size, _ = lax.while_loop(going, advance, (0, start[0, 0], start))

    @pl.when(size > limit)
    def _():
        r[...] = b

        @pl.loop(0, m)
        def _(k):
            lane = lax.broadcasted_iota(jnp.int32, (m, m), 1)
            line = lax.broadcasted_iota(jnp.int32, (m, m), 0)
            here = matrix[...]
            row = matrix[pl.ds(k, 1), :]
            value = r[pl.ds(k, 1), :]
            column = jnp.sum(jnp.where(lane == k, here, 0.0), axis=1, keepdims=True)
            pivot = jnp.sum(jnp.where(lane[0:1] == k, row, 0.0), axis=1, keepdims=True)
            factor = jnp.where(line == k, 0.0, column / pivot)
            matrix[...] = here - factor * row
            r[...] = r[...] - factor * value

        x[...] = r[...] / jnp.broadcast_to(
            jnp.sum(jnp.where(eye, matrix[...], 0.0), axis=1, keepdims=True), (m, m)
        )

    found = scale * x[...]
    x[...] = found
    coefficients_ref[...] = as_row(found, eye)
    lines = correction_ref.shape[0]
    totals = [jnp.zeros((lines, LANES), jnp.float32) for _ in range(2)]
    for k in range(m):
        totals[k % 2] += diffs_ref[k] * x[k : k + 1, :]
    correction_ref[...] = totals[0] + totals[1]


def local_sums(res_diffs, residual, lines):
    m = res_diffs.shape[0]
    diffs = rows_of(res_diffs)
    rows = diffs.shape[1]
    return pl.pallas_call(
        gram_kernel,
        out_shape=pltpu.VMEM((lines, LANES), jnp.float32),
        in_specs=[pl.BlockSpec(memory_space=pl.ANY), pl.BlockSpec(memory_space=pltpu.VMEM)],
        out_specs=pl.BlockSpec(memory_space=pltpu.VMEM),
        scratch_shapes=[
            pltpu.VMEM((rows // SUBLANES, m, SUBLANES, LANES), jnp.float32),
            pltpu.SemaphoreType.DMA((rows // SUBLANES,)),
        ],
        name="gram",
    )(diffs, rows_of(residual))


def solve_and_apply(sums, diffs, rows_all):
    m, lines = diffs.shape[:2]
    square = pltpu.VMEM((m, LANES), jnp.float32)
    correction, coefficients = pl.pallas_call(
        lambda *refs: solve_kernel(rows_all, *refs),
        out_shape=(
            jax.ShapeDtypeStruct((lines, LANES), jnp.float32),
            jax.ShapeDtypeStruct((1, m), jnp.float32),
        ),
        in_specs=[pl.BlockSpec(memory_space=pltpu.VMEM), pl.BlockSpec(memory_space=pltpu.VMEM)],
        out_specs=(pl.BlockSpec(memory_space=pltpu.VMEM), pl.BlockSpec(memory_space=pltpu.VMEM)),
        scratch_shapes=[square, square, square, square],
        name="solve",
    )(pltpu.with_memory_space_constraint(sums, pltpu.VMEM), diffs)
    blocks = correction.reshape(lines // 2, 2, LANES)
    return jnp.swapaxes(blocks, 0, 1).reshape(2, -1), coefficients.reshape(m)


def exchange(chunks, groups):
    return lax.all_to_all(chunks, AXIS, 0, 0, axis_index_groups=groups)


def on_device(res_diffs, out_diffs, residual):
    rows_all = residual.shape[1] * lax.axis_size(AXIS)
    inner = groups_over(INNER)
    pieces = len(inner[0])
    lines = -(-133 // pieces) * pieces
    sums = local_sums(res_diffs, residual, lines)
    sums, out_diffs = lax.optimization_barrier((sums, out_diffs))
    fetched = pltpu.with_memory_space_constraint(rows_of(out_diffs), pltpu.VMEM)
    part = jnp.sum(exchange(sums.reshape(pieces, 1, -1), inner), axis=0)
    for names in STEPS:
        groups = groups_over(names)
        part = jnp.sum(exchange(jnp.broadcast_to(part, (len(groups[0]),) + part.shape), groups), axis=0)
    whole = exchange(jnp.broadcast_to(part, (pieces,) + part.shape), inner)
    return solve_and_apply(whole.reshape(lines, LANES), fetched, rows_all)


def solution(mesh):
    placed = (P(None, None, AXIS), P(None, None, AXIS), P(None, AXIS))
    return jax.shard_map(
        on_device, mesh=mesh, in_specs=placed, out_specs=(P(None, AXIS), P()), check_vma=False
    )
```

```python
import jax
import jax.numpy as jnp
from jax import lax
from jax.experimental import pallas as pl
from jax.experimental.pallas import tpu as pltpu
from jax.sharding import PartitionSpec as P

AXIS = "iface"
LANES = 128
SUBLANES = 8
EPSILON = 1e-06
TOLERANCE = 1e-06
STEPS_MAX = 16
INNER = ('y0', 'x1', 'x0', 'c')
STEPS = [('y2', 'y1', 'z2', 'z1', 'z0')]
ROOT = ('y0', 'x1', 'y2', 'z2')
BITS = ("y2", "y1", "y0", "z2", "z1", "z0", "x1", "x0", "c")


def groups_over(names):
    count = len(BITS)
    root = sum(1 << (count - 1 - BITS.index(name)) for name in names if name in ROOT)
    found = {}
    for device in range(1 << count):
        bits = [((device ^ root) >> (count - 1 - k)) & 1 for k in range(count)]
        key = tuple(b for b, name in zip(bits, BITS) if name not in names)
        found.setdefault(key, []).append(device)
    return [sorted(group, key=lambda device: device ^ root) for group in found.values()]


def rows_of(x):
    lead = x.shape[:-2]
    fields, n = x.shape[-2:]
    blocks = x.reshape(lead + (fields, n // LANES, LANES))
    return jnp.swapaxes(blocks, -3, -2).reshape(lead + (fields * n // LANES, LANES))


def eye_mask(m):
    return lax.broadcasted_iota(jnp.int32, (m, m), 0) == lax.broadcasted_iota(jnp.int32, (m, m), 1)


def as_row(column, eye):
    return jnp.sum(jnp.where(eye, column, 0.0), axis=0, keepdims=True)


def as_column(row, eye):
    m = eye.shape[0]
    return jnp.broadcast_to(jnp.sum(jnp.where(eye, row, 0.0), axis=1, keepdims=True), (m, m))


def split(x):
    high = x.astype(jnp.bfloat16)
    rest = x - high.astype(jnp.float32)
    middle = rest.astype(jnp.bfloat16)
    return high, middle, (rest - middle.astype(jnp.float32)).astype(jnp.bfloat16)


def gram_kernel(diffs_ref, given_ref, out_ref, staged, residual_ref, sems):
    m, rows = diffs_ref.shape[:2]
    tiles = rows // SUBLANES
    first = pltpu.make_async_copy(given_ref, residual_ref, sems.at[tiles])
    first.start()
    copies = [
        pltpu.make_async_copy(
            diffs_ref.at[:, t * SUBLANES : (t + 1) * SUBLANES, :], staged.at[t], sems.at[t]
        )
        for t in range(tiles)
    ]
    for copy in copies:
        copy.start()
    eye = eye_mask(m)
    first.wait()
    residual = residual_ref[...]
    parity = lax.broadcasted_iota(jnp.int32, residual.shape, 0) & 1
    squares = []
    for f in range(2):
        own = jnp.where(parity == f, residual * residual, 0.0)
        total = jnp.sum(jnp.sum(own, axis=0, keepdims=True), axis=1, keepdims=True)
        squares.append(jnp.broadcast_to(total, (1, LANES)))
    projs = [jnp.zeros((m, LANES), jnp.float32)] * 2
    products = [jnp.zeros((3 * m, 2 * m), jnp.float32)] * 2
    for t in range(tiles):
        copies[t].wait()
        lines = staged.at[t].reshape(m * SUBLANES, LANES)
        for f in range(2):
            parts = []
            for s in range(f, SUBLANES, 2):
                block = lines[pl.ds(s, m, stride=SUBLANES), :]
                row = t * SUBLANES + s
                projs[f] = projs[f] + block * residual_ref[row : row + 1, :]
                parts.append(split(block))
            high, middle, low = (jnp.concatenate(part, axis=1) for part in zip(*parts))
            products[f] = products[f] + lax.dot_general(
                jnp.concatenate([high, middle, low], axis=0),
                jnp.concatenate([high, middle], axis=0),
                (((1,), (1,)), ((), ())),
                preferred_element_type=jnp.float32,
            )
    grams = []
    for product in products:
        cross = product[2 * m :, 0:m]
        small = product[m : 2 * m, m:] + (cross + cross.T)
        grams.append(product[0:m, 0:m] + (small + (product[0:m, m:] + product[m : 2 * m, 0:m])))
    below = lax.broadcasted_iota(jnp.int32, (m, m), 0) > lax.broadcasted_iota(jnp.int32, (m, m), 1)
    out_ref[0:m, :] = jnp.where(below, grams[0], grams[1])
    lines = [as_row(jnp.sum(proj, axis=1, keepdims=True), eye) for proj in projs]
    lines += [as_row(grams[0], eye), *squares]
    at = lax.broadcasted_iota(jnp.int32, (out_ref.shape[0] - m, LANES), 0)
    extra = jnp.zeros(at.shape, jnp.float32)
    for i, line in enumerate(lines):
        extra = jnp.where(at == i, line, extra)
    out_ref[m:, :] = extra


def solve_kernel(rows_all, sums_ref, diffs_ref, correction_ref, coefficients_ref, matrix, x, r, p):
    m = diffs_ref.shape[0]
    eye = eye_mask(m)
    below = lax.broadcasted_iota(jnp.int32, (m, m), 0) > lax.broadcasted_iota(jnp.int32, (m, m), 1)
    packed = sums_ref[0:m, :]
    extra = sums_ref[m : m + 8, :]
    w0 = 1.0 / (extra[3:4, :] / rows_all + EPSILON)
    w1 = 1.0 / (extra[4:5, :] / rows_all + EPSILON)
    turned = packed.T
    gram = jnp.where(below, w0 * packed + w1 * turned, w1 * packed + w0 * turned)
    gram = jnp.where(eye, w1 * packed + w0 * extra[2:3, :], gram)
    b_row = -(w0 * extra[0:1, :] + w1 * extra[1:2, :])
    only = jnp.where(eye, gram, 0.0)
    scale_row = lax.rsqrt(jnp.sum(only, axis=0, keepdims=True))
    scale = lax.rsqrt(jnp.broadcast_to(jnp.sum(only, axis=1, keepdims=True), (m, m)))
    matrix[...] = (scale * gram) * scale_row
    b = as_column(b_row * scale_row, eye)
    x[...] = jnp.zeros((m, m), jnp.float32)
    r[...] = b
    p[...] = b

    def dot(u, v):
        return jnp.sum(u * v, axis=0, keepdims=True)

    def ratio(top, bottom):
        return jnp.where(bottom > 0.0, top / jnp.where(bottom > 0.0, bottom, 1.0), 0.0)

    start = dot(b, b)
    limit = start[0, 0] * (TOLERANCE * TOLERANCE)

    def going(state):
        step, size, _ = state
        return (step < STEPS_MAX) & (size > limit)

    def advance(state):
        step, _, rr = state
        direction = p[...]
        image = jnp.broadcast_to(
            jnp.sum(matrix[...] * as_row(direction, eye), axis=1, keepdims=True), (m, m)
        )
        alpha = ratio(rr, dot(direction, image))
        x[...] += alpha * direction
        rest = r[...] - alpha * image
        r[...] = rest
        after = dot(rest, rest)
        p[...] = rest + ratio(after, rr) * direction
        return step + 1, after[0, 0], after

    _, size, _ = lax.while_loop(going, advance, (0, start[0, 0], start))

    @pl.when(size > limit)
    def _():
        r[...] = b

        @pl.loop(0, m)
        def _(k):
            lane = lax.broadcasted_iota(jnp.int32, (m, m), 1)
            line = lax.broadcasted_iota(jnp.int32, (m, m), 0)
            here = matrix[...]
            row = matrix[pl.ds(k, 1), :]
            value = r[pl.ds(k, 1), :]
            column = jnp.sum(jnp.where(lane == k, here, 0.0), axis=1, keepdims=True)
            pivot = jnp.sum(jnp.where(lane[0:1] == k, row, 0.0), axis=1, keepdims=True)
            factor = jnp.where(line == k, 0.0, column / pivot)
            matrix[...] = here - factor * row
            r[...] = r[...] - factor * value

        x[...] = r[...] / jnp.broadcast_to(
            jnp.sum(jnp.where(eye, matrix[...], 0.0), axis=1, keepdims=True), (m, m)
        )

    found = scale * x[...]
    x[...] = found
    coefficients_ref[...] = as_row(found, eye)
    lines = correction_ref.shape[0]
    totals = [jnp.zeros((lines, LANES), jnp.float32) for _ in range(2)]
    for k in range(m):
        totals[k % 2] += diffs_ref[k] * x[k : k + 1, :]
    correction_ref[...] = totals[0] + totals[1]


def local_sums(res_diffs, residual, lines):
    m = res_diffs.shape[0]
    diffs = rows_of(res_diffs)
    rows = diffs.shape[1]
    return pl.pallas_call(
        gram_kernel,
        out_shape=pltpu.VMEM((lines, LANES), jnp.float32),
        in_specs=[pl.BlockSpec(memory_space=pl.ANY), pl.BlockSpec(memory_space=pl.ANY)],
        out_specs=pl.BlockSpec(memory_space=pltpu.VMEM),
        scratch_shapes=[
            pltpu.VMEM((rows // SUBLANES, m, SUBLANES, LANES), jnp.float32),
            pltpu.VMEM((rows, LANES), jnp.float32),
            pltpu.SemaphoreType.DMA((rows // SUBLANES + 1,)),
        ],
        name="gram",
    )(diffs, rows_of(residual))


def solve_and_apply(sums, diffs, rows_all):
    m, lines = diffs.shape[:2]
    square = pltpu.VMEM((m, LANES), jnp.float32)
    correction, coefficients = pl.pallas_call(
        lambda *refs: solve_kernel(rows_all, *refs),
        out_shape=(
            jax.ShapeDtypeStruct((lines, LANES), jnp.float32),
            jax.ShapeDtypeStruct((1, m), jnp.float32),
        ),
        in_specs=[pl.BlockSpec(memory_space=pltpu.VMEM), pl.BlockSpec(memory_space=pltpu.VMEM)],
        out_specs=(pl.BlockSpec(memory_space=pltpu.VMEM), pl.BlockSpec(memory_space=pltpu.VMEM)),
        scratch_shapes=[square, square, square, square],
        name="solve",
    )(pltpu.with_memory_space_constraint(sums, pltpu.VMEM), diffs)
    blocks = correction.reshape(lines // 2, 2, LANES)
    return jnp.swapaxes(blocks, 0, 1).reshape(2, -1), coefficients.reshape(m)


def exchange(chunks, groups):
    return lax.all_to_all(chunks, AXIS, 0, 0, axis_index_groups=groups)


def on_device(res_diffs, out_diffs, residual):
    rows_all = residual.shape[1] * lax.axis_size(AXIS)
    inner = groups_over(INNER)
    pieces = len(inner[0])
    lines = -(-133 // pieces) * pieces
    sums = local_sums(res_diffs, residual, lines)
    sums, out_diffs = lax.optimization_barrier((sums, out_diffs))
    fetched = pltpu.with_memory_space_constraint(rows_of(out_diffs), pltpu.VMEM)
    part = jnp.sum(exchange(sums.reshape(pieces, 1, -1), inner), axis=0)
    for names in STEPS:
        groups = groups_over(names)
        part = jnp.sum(exchange(jnp.broadcast_to(part, (len(groups[0]),) + part.shape), groups), axis=0)
    whole = exchange(jnp.broadcast_to(part, (pieces,) + part.shape), inner)
    return solve_and_apply(whole.reshape(lines, LANES), fetched, rows_all)


def solution(mesh):
    placed = (P(None, None, AXIS), P(None, None, AXIS), P(None, AXIS))
    return jax.shard_map(
        on_device, mesh=mesh, in_specs=placed, out_specs=(P(None, AXIS), P()), check_vma=False
    )
```

```python
import jax
import jax.numpy as jnp
from jax import lax
from jax.experimental import pallas as pl
from jax.experimental.pallas import tpu as pltpu
from jax.sharding import PartitionSpec as P

AXIS = "iface"
LANES = 128
SUBLANES = 8
EPSILON = 1e-06
TOLERANCE = 1e-06
STEPS_MAX = 16
INNER = ('z0', 'x1', 'x0', 'c')
STEPS = [('y2', 'y1', 'y0', 'z2', 'z1')]
ROOT = ('z0', 'x1', 'c', 'y2', 'z2')
BITS = ("y2", "y1", "y0", "z2", "z1", "z0", "x1", "x0", "c")


def groups_over(names):
    count = len(BITS)
    root = sum(1 << (count - 1 - BITS.index(name)) for name in names if name in ROOT)
    found = {}
    for device in range(1 << count):
        bits = [((device ^ root) >> (count - 1 - k)) & 1 for k in range(count)]
        key = tuple(b for b, name in zip(bits, BITS) if name not in names)
        found.setdefault(key, []).append(device)
    return [[group[0] ^ root] + [d for d in group if d != group[0] ^ root] for group in map(sorted, found.values())]


def rows_of(x):
    lead = x.shape[:-2]
    fields, n = x.shape[-2:]
    blocks = x.reshape(lead + (fields, n // LANES, LANES))
    return jnp.swapaxes(blocks, -3, -2).reshape(lead + (fields * n // LANES, LANES))


def eye_mask(m):
    return lax.broadcasted_iota(jnp.int32, (m, m), 0) == lax.broadcasted_iota(jnp.int32, (m, m), 1)


def as_row(column, eye):
    return jnp.sum(jnp.where(eye, column, 0.0), axis=0, keepdims=True)


def as_column(row, eye):
    m = eye.shape[0]
    return jnp.broadcast_to(jnp.sum(jnp.where(eye, row, 0.0), axis=1, keepdims=True), (m, m))


def split(x):
    high = x.astype(jnp.bfloat16)
    rest = x - high.astype(jnp.float32)
    middle = rest.astype(jnp.bfloat16)
    return high, middle, (rest - middle.astype(jnp.float32)).astype(jnp.bfloat16)


def gram_kernel(diffs_ref, given_ref, out_ref, staged, residual_ref, sems):
    m, rows = diffs_ref.shape[:2]
    tiles = rows // SUBLANES
    first = pltpu.make_async_copy(given_ref, residual_ref, sems.at[tiles])
    first.start()
    copies = [
        pltpu.make_async_copy(
            diffs_ref.at[:, t * SUBLANES : (t + 1) * SUBLANES, :], staged.at[t], sems.at[t]
        )
        for t in range(tiles)
    ]
    for copy in copies:
        copy.start()
    eye = eye_mask(m)
    first.wait()
    residual = residual_ref[...]
    parity = lax.broadcasted_iota(jnp.int32, residual.shape, 0) & 1
    squares = []
    for f in range(2):
        own = jnp.where(parity == f, residual * residual, 0.0)
        total = jnp.sum(jnp.sum(own, axis=0, keepdims=True), axis=1, keepdims=True)
        squares.append(jnp.broadcast_to(total, (1, LANES)))
    projs = [jnp.zeros((m, LANES), jnp.float32)] * 2
    products = [jnp.zeros((3 * m, 2 * m), jnp.float32)] * 2
    for t in range(tiles):
        copies[t].wait()
        lines = staged.at[t].reshape(m * SUBLANES, LANES)
        for f in range(2):
            parts = []
            for s in range(f, SUBLANES, 2):
                block = lines[pl.ds(s, m, stride=SUBLANES), :]
                row = t * SUBLANES + s
                projs[f] = projs[f] + block * residual_ref[row : row + 1, :]
                parts.append(split(block))
            high, middle, low = (jnp.concatenate(part, axis=1) for part in zip(*parts))
            products[f] = products[f] + lax.dot_general(
                jnp.concatenate([high, middle, low], axis=0),
                jnp.concatenate([high, middle], axis=0),
                (((1,), (1,)), ((), ())),
                preferred_element_type=jnp.float32,
            )
    grams = []
    for product in products:
        cross = product[2 * m :, 0:m]
        small = product[m : 2 * m, m:] + (cross + cross.T)
        grams.append(product[0:m, 0:m] + (small + (product[0:m, m:] + product[m : 2 * m, 0:m])))
    below = lax.broadcasted_iota(jnp.int32, (m, m), 0) > lax.broadcasted_iota(jnp.int32, (m, m), 1)
    out_ref[0:m, :] = jnp.where(below, grams[0], grams[1])
    lines = [as_row(jnp.sum(proj, axis=1, keepdims=True), eye) for proj in projs]
    lines += [as_row(grams[0], eye), *squares]
    at = lax.broadcasted_iota(jnp.int32, (out_ref.shape[0] - m, LANES), 0)
    extra = jnp.zeros(at.shape, jnp.float32)
    for i, line in enumerate(lines):
        extra = jnp.where(at == i, line, extra)
    out_ref[m:, :] = extra


def solve_kernel(rows_all, sums_ref, diffs_ref, correction_ref, coefficients_ref, matrix, x, r, p):
    m = diffs_ref.shape[0]
    eye = eye_mask(m)
    below = lax.broadcasted_iota(jnp.int32, (m, m), 0) > lax.broadcasted_iota(jnp.int32, (m, m), 1)
    packed = sums_ref[0:m, :]
    extra = sums_ref[m : m + 8, :]
    w0 = 1.0 / (extra[3:4, :] / rows_all + EPSILON)
    w1 = 1.0 / (extra[4:5, :] / rows_all + EPSILON)
    turned = packed.T
    gram = jnp.where(below, w0 * packed + w1 * turned, w1 * packed + w0 * turned)
    gram = jnp.where(eye, w1 * packed + w0 * extra[2:3, :], gram)
    b_row = -(w0 * extra[0:1, :] + w1 * extra[1:2, :])
    only = jnp.where(eye, gram, 0.0)
    scale_row = lax.rsqrt(jnp.sum(only, axis=0, keepdims=True))
    scale = lax.rsqrt(jnp.broadcast_to(jnp.sum(only, axis=1, keepdims=True), (m, m)))
    matrix[...] = (scale * gram) * scale_row
    b = as_column(b_row * scale_row, eye)
    x[...] = jnp.zeros((m, m), jnp.float32)
    r[...] = b
    p[...] = b

    def dot(u, v):
        return jnp.sum(u * v, axis=0, keepdims=True)

    def ratio(top, bottom):
        return jnp.where(bottom > 0.0, top / jnp.where(bottom > 0.0, bottom, 1.0), 0.0)

    start = dot(b, b)
    limit = start[0, 0] * (TOLERANCE * TOLERANCE)

    def going(state):
        step, size, _ = state
        return (step < STEPS_MAX) & (size > limit)

    def advance(state):
        step, _, rr = state
        direction = p[...]
        image = jnp.broadcast_to(
            jnp.sum(matrix[...] * as_row(direction, eye), axis=1, keepdims=True), (m, m)
        )
        alpha = ratio(rr, dot(direction, image))
        x[...] += alpha * direction
        rest = r[...] - alpha * image
        r[...] = rest
        after = dot(rest, rest)
        p[...] = rest + ratio(after, rr) * direction
        return step + 1, after[0, 0], after

    _, size, _ = lax.while_loop(going, advance, (0, start[0, 0], start))

    @pl.when(size > limit)
    def _():
        r[...] = b

        @pl.loop(0, m)
        def _(k):
            lane = lax.broadcasted_iota(jnp.int32, (m, m), 1)
            line = lax.broadcasted_iota(jnp.int32, (m, m), 0)
            here = matrix[...]
            row = matrix[pl.ds(k, 1), :]
            value = r[pl.ds(k, 1), :]
            column = jnp.sum(jnp.where(lane == k, here, 0.0), axis=1, keepdims=True)
            pivot = jnp.sum(jnp.where(lane[0:1] == k, row, 0.0), axis=1, keepdims=True)
            factor = jnp.where(line == k, 0.0, column / pivot)
            matrix[...] = here - factor * row
            r[...] = r[...] - factor * value

        x[...] = r[...] / jnp.broadcast_to(
            jnp.sum(jnp.where(eye, matrix[...], 0.0), axis=1, keepdims=True), (m, m)
        )

    found = scale * x[...]
    x[...] = found
    coefficients_ref[...] = as_row(found, eye)
    lines = correction_ref.shape[0]
    totals = [jnp.zeros((lines, LANES), jnp.float32) for _ in range(2)]
    for k in range(m):
        totals[k % 2] += diffs_ref[k] * x[k : k + 1, :]
    correction_ref[...] = totals[0] + totals[1]


def local_sums(res_diffs, residual, lines):
    m = res_diffs.shape[0]
    diffs = rows_of(res_diffs)
    rows = diffs.shape[1]
    return pl.pallas_call(
        gram_kernel,
        out_shape=pltpu.VMEM((lines, LANES), jnp.float32),
        in_specs=[pl.BlockSpec(memory_space=pl.ANY), pl.BlockSpec(memory_space=pl.ANY)],
        out_specs=pl.BlockSpec(memory_space=pltpu.VMEM),
        scratch_shapes=[
            pltpu.VMEM((rows // SUBLANES, m, SUBLANES, LANES), jnp.float32),
            pltpu.VMEM((rows, LANES), jnp.float32),
            pltpu.SemaphoreType.DMA((rows // SUBLANES + 1,)),
        ],
        name="gram",
    )(diffs, rows_of(residual))


def solve_and_apply(sums, diffs, rows_all):
    m, lines = diffs.shape[:2]
    square = pltpu.VMEM((m, LANES), jnp.float32)
    correction, coefficients = pl.pallas_call(
        lambda *refs: solve_kernel(rows_all, *refs),
        out_shape=(
            jax.ShapeDtypeStruct((lines, LANES), jnp.float32),
            jax.ShapeDtypeStruct((1, m), jnp.float32),
        ),
        in_specs=[pl.BlockSpec(memory_space=pltpu.VMEM), pl.BlockSpec(memory_space=pltpu.VMEM)],
        out_specs=(pl.BlockSpec(memory_space=pltpu.VMEM), pl.BlockSpec(memory_space=pltpu.VMEM)),
        scratch_shapes=[square, square, square, square],
        name="solve",
    )(pltpu.with_memory_space_constraint(sums, pltpu.VMEM), diffs)
    blocks = correction.reshape(lines // 2, 2, LANES)
    return jnp.swapaxes(blocks, 0, 1).reshape(2, -1), coefficients.reshape(m)


def exchange(chunks, groups):
    return lax.all_to_all(chunks, AXIS, 0, 0, axis_index_groups=groups)


def on_device(res_diffs, out_diffs, residual):
    rows_all = residual.shape[1] * lax.axis_size(AXIS)
    inner = groups_over(INNER)
    pieces = len(inner[0])
    lines = -(-133 // pieces) * pieces
    sums = local_sums(res_diffs, residual, lines)
    sums, out_diffs = lax.optimization_barrier((sums, out_diffs))
    fetched = pltpu.with_memory_space_constraint(rows_of(out_diffs), pltpu.VMEM)
    part = jnp.sum(exchange(sums.reshape(pieces, 1, -1), inner), axis=0)
    for names in STEPS:
        groups = groups_over(names)
        part = jnp.sum(exchange(jnp.broadcast_to(part, (len(groups[0]),) + part.shape), groups), axis=0)
    whole = exchange(jnp.broadcast_to(part, (pieces,) + part.shape), inner)
    return solve_and_apply(whole.reshape(lines, LANES), fetched, rows_all)


def solution(mesh):
    placed = (P(None, None, AXIS), P(None, None, AXIS), P(None, AXIS))
    return jax.shard_map(
        on_device, mesh=mesh, in_specs=placed, out_specs=(P(None, AXIS), P()), check_vma=False
    )
```

```python
import jax
import jax.numpy as jnp
from jax import lax
from jax.experimental import pallas as pl
from jax.experimental.pallas import tpu as pltpu
from jax.sharding import PartitionSpec as P

AXIS = "iface"
LANES = 128
SUBLANES = 8
EPSILON = 1e-06
TOLERANCE = 1e-06
STEPS_PER_TEST = 4
TESTS_MAX = 4
INNER = ('z0', 'x1', 'x0', 'c')
STEPS = [('y2', 'y1', 'y0', 'z2', 'z1')]
ROOT = ('z0', 'x1', 'c', 'y2', 'z2')
BITS = ("y2", "y1", "y0", "z2", "z1", "z0", "x1", "x0", "c")


def groups_over(names):
    count = len(BITS)
    root = sum(1 << (count - 1 - BITS.index(name)) for name in names if name in ROOT)
    found = {}
    for device in range(1 << count):
        bits = [((device ^ root) >> (count - 1 - k)) & 1 for k in range(count)]
        key = tuple(b for b, name in zip(bits, BITS) if name not in names)
        found.setdefault(key, []).append(device)
    return [[group[0] ^ root] + [d for d in group if d != group[0] ^ root] for group in map(sorted, found.values())]


def rows_of(x):
    lead = x.shape[:-2]
    fields, n = x.shape[-2:]
    blocks = x.reshape(lead + (fields, n // LANES, LANES))
    return jnp.swapaxes(blocks, -3, -2).reshape(lead + (fields * n // LANES, LANES))


def eye_mask(m):
    return lax.broadcasted_iota(jnp.int32, (m, m), 0) == lax.broadcasted_iota(jnp.int32, (m, m), 1)


def as_row(column, eye):
    return jnp.sum(jnp.where(eye, column, 0.0), axis=0, keepdims=True)


def as_column(row, eye):
    m = eye.shape[0]
    return jnp.broadcast_to(jnp.sum(jnp.where(eye, row, 0.0), axis=1, keepdims=True), (m, m))


def split(x):
    high = x.astype(jnp.bfloat16)
    rest = x - high.astype(jnp.float32)
    middle = rest.astype(jnp.bfloat16)
    return high, middle, (rest - middle.astype(jnp.float32)).astype(jnp.bfloat16)


def gram_kernel(diffs_ref, given_ref, out_ref, staged, residual_ref, products, sems):
    m, rows = diffs_ref.shape[:2]
    tiles = rows // SUBLANES
    first = pltpu.make_async_copy(given_ref, residual_ref, sems.at[tiles])
    first.start()
    copies = [
        pltpu.make_async_copy(
            diffs_ref.at[:, t * SUBLANES : (t + 1) * SUBLANES, :], staged.at[t], sems.at[t]
        )
        for t in range(tiles)
    ]
    for copy in copies:
        copy.start()
    eye = eye_mask(m)
    first.wait()
    residual = residual_ref[...]
    parity = lax.broadcasted_iota(jnp.int32, residual.shape, 0) & 1
    squares = []
    for f in range(2):
        own = jnp.where(parity == f, residual * residual, 0.0)
        total = jnp.sum(jnp.sum(own, axis=0, keepdims=True), axis=1, keepdims=True)
        squares.append(jnp.broadcast_to(total, (1, LANES)))
    projs = [jnp.zeros((m, LANES), jnp.float32)] * 2
    for t in range(tiles):
        copies[t].wait()
        lines = staged.at[t].reshape(m * SUBLANES, LANES)
        for f in range(2):
            parts = []
            for s in range(f, SUBLANES, 2):
                block = lines[pl.ds(s, m, stride=SUBLANES), :]
                row = t * SUBLANES + s
                projs[f] = projs[f] + block * residual_ref[row : row + 1, :]
                parts.append(split(block))
            high, middle, low = (jnp.concatenate(part, axis=1) for part in zip(*parts))
            product = lax.dot_general(
                jnp.concatenate([high, middle, low], axis=0),
                jnp.concatenate([high, middle], axis=0),
                (((1,), (1,)), ((), ())),
                preferred_element_type=jnp.float32,
            )
            products[f] = product if t == 0 else products[f] + product
    grams = []
    for f in range(2):
        product = products[f]
        cross = product[2 * m :, 0:m]
        small = product[m : 2 * m, m:] + (cross + cross.T)
        grams.append(product[0:m, 0:m] + (small + (product[0:m, m:] + product[m : 2 * m, 0:m])))
    below = lax.broadcasted_iota(jnp.int32, (m, m), 0) > lax.broadcasted_iota(jnp.int32, (m, m), 1)
    out_ref[0:m, :] = jnp.where(below, grams[0], grams[1])
    lines = [as_row(jnp.sum(proj, axis=1, keepdims=True), eye) for proj in projs]
    lines += [as_row(grams[0], eye), *squares]
    at = lax.broadcasted_iota(jnp.int32, (out_ref.shape[0] - m, LANES), 0)
    extra = jnp.zeros(at.shape, jnp.float32)
    for i, line in enumerate(lines):
        extra = jnp.where(at == i, line, extra)
    out_ref[m:, :] = extra


def solve_kernel(rows_all, sums_ref, diffs_ref, correction_ref, coefficients_ref, matrix, x, r, p):
    m = diffs_ref.shape[0]
    eye = eye_mask(m)
    below = lax.broadcasted_iota(jnp.int32, (m, m), 0) > lax.broadcasted_iota(jnp.int32, (m, m), 1)
    packed = sums_ref[0:m, :]
    extra = sums_ref[m : m + 8, :]
    w0 = 1.0 / (extra[3:4, :] / rows_all + EPSILON)
    w1 = 1.0 / (extra[4:5, :] / rows_all + EPSILON)
    turned = packed.T
    gram = jnp.where(below, w0 * packed + w1 * turned, w1 * packed + w0 * turned)
    gram = jnp.where(eye, w1 * packed + w0 * extra[2:3, :], gram)
    b_row = -(w0 * extra[0:1, :] + w1 * extra[1:2, :])
    only = jnp.where(eye, gram, 0.0)
    scale_row = lax.rsqrt(jnp.sum(only, axis=0, keepdims=True))
    scale = lax.rsqrt(jnp.broadcast_to(jnp.sum(only, axis=1, keepdims=True), (m, m)))
    matrix[...] = (scale * gram) * scale_row
    b = as_column(b_row * scale_row, eye)
    x[...] = jnp.zeros((m, m), jnp.float32)
    r[...] = b
    p[...] = b

    def dot(u, v):
        return jnp.sum(u * v, axis=0, keepdims=True)

    def ratio(top, bottom):
        return jnp.where(bottom > 0.0, top / jnp.where(bottom > 0.0, bottom, 1.0), 0.0)

    start = dot(b, b)
    limit = start * (TOLERANCE * TOLERANCE)

    def advance(rr):
        for _ in range(STEPS_PER_TEST):
            direction = p[...]
            image = jnp.broadcast_to(
                jnp.sum(matrix[...] * as_row(direction, eye), axis=1, keepdims=True), (m, m)
            )
            alpha = ratio(rr, dot(direction, image))
            x[...] += alpha * direction
            rest = r[...] - alpha * image
            r[...] = rest
            after = dot(rest, rest)
            p[...] = rest + ratio(after, rr) * direction
            rr = after
        return (rr - limit)[0, 0], rr

    over, rr = advance(start)
    _, over, _ = lax.while_loop(
        lambda state: (state[0] < TESTS_MAX) & (state[1] > 0.0),
        lambda state: (state[0] + 1, *advance(state[2])),
        (1, over, rr),
    )

    @pl.when(over > 0.0)
    def _():
        r[...] = b

        @pl.loop(0, m)
        def _(k):
            lane = lax.broadcasted_iota(jnp.int32, (m, m), 1)
            line = lax.broadcasted_iota(jnp.int32, (m, m), 0)
            here = matrix[...]
            row = matrix[pl.ds(k, 1), :]
            value = r[pl.ds(k, 1), :]
            column = jnp.sum(jnp.where(lane == k, here, 0.0), axis=1, keepdims=True)
            pivot = jnp.sum(jnp.where(lane[0:1] == k, row, 0.0), axis=1, keepdims=True)
            factor = jnp.where(line == k, 0.0, column / pivot)
            matrix[...] = here - factor * row
            r[...] = r[...] - factor * value

        x[...] = r[...] / jnp.broadcast_to(
            jnp.sum(jnp.where(eye, matrix[...], 0.0), axis=1, keepdims=True), (m, m)
        )

    found = scale * x[...]
    x[...] = found
    coefficients_ref[...] = as_row(found, eye)
    lines = correction_ref.shape[0]
    totals = [jnp.zeros((lines, LANES), jnp.float32) for _ in range(2)]
    for k in range(m):
        totals[k % 2] += diffs_ref[k] * x[k : k + 1, :]
    correction_ref[...] = totals[0] + totals[1]


def local_sums(res_diffs, residual, lines):
    m = res_diffs.shape[0]
    diffs = rows_of(res_diffs)
    rows = diffs.shape[1]
    return pl.pallas_call(
        gram_kernel,
        out_shape=pltpu.VMEM((lines, LANES), jnp.float32),
        in_specs=[pl.BlockSpec(memory_space=pl.ANY), pl.BlockSpec(memory_space=pl.ANY)],
        out_specs=pl.BlockSpec(memory_space=pltpu.VMEM),
        scratch_shapes=[
            pltpu.VMEM((rows // SUBLANES, m, SUBLANES, LANES), jnp.float32),
            pltpu.VMEM((rows, LANES), jnp.float32),
            pltpu.VMEM((2, 3 * m, 2 * m), jnp.float32),
            pltpu.SemaphoreType.DMA((rows // SUBLANES + 1,)),
        ],
        name="gram",
    )(diffs, rows_of(residual))


def solve_and_apply(sums, diffs, rows_all):
    m, lines = diffs.shape[:2]
    square = pltpu.VMEM((m, LANES), jnp.float32)
    correction, coefficients = pl.pallas_call(
        lambda *refs: solve_kernel(rows_all, *refs),
        out_shape=(
            jax.ShapeDtypeStruct((lines, LANES), jnp.float32),
            jax.ShapeDtypeStruct((1, m), jnp.float32),
        ),
        in_specs=[pl.BlockSpec(memory_space=pltpu.VMEM), pl.BlockSpec(memory_space=pltpu.VMEM)],
        out_specs=(pl.BlockSpec(memory_space=pltpu.VMEM), pl.BlockSpec(memory_space=pltpu.VMEM)),
        scratch_shapes=[square, square, square, square],
        name="solve",
    )(pltpu.with_memory_space_constraint(sums, pltpu.VMEM), diffs)
    blocks = correction.reshape(lines // 2, 2, LANES)
    return jnp.swapaxes(blocks, 0, 1).reshape(2, -1), coefficients.reshape(m)


def exchange(chunks, groups):
    return lax.all_to_all(chunks, AXIS, 0, 0, axis_index_groups=groups)


def on_device(res_diffs, out_diffs, residual):
    rows_all = residual.shape[1] * lax.axis_size(AXIS)
    inner = groups_over(INNER)
    pieces = len(inner[0])
    lines = -(-133 // pieces) * pieces
    sums = local_sums(res_diffs, residual, lines)
    sums, out_diffs = lax.optimization_barrier((sums, out_diffs))
    fetched = pltpu.with_memory_space_constraint(rows_of(out_diffs), pltpu.VMEM)
    part = jnp.sum(exchange(sums.reshape(pieces, 1, -1), inner), axis=0)
    for names in STEPS:
        groups = groups_over(names)
        part = jnp.sum(exchange(jnp.broadcast_to(part, (len(groups[0]),) + part.shape), groups), axis=0)
    whole = exchange(jnp.broadcast_to(part, (pieces,) + part.shape), inner)
    return solve_and_apply(whole.reshape(lines, LANES), fetched, rows_all)


def solution(mesh):
    placed = (P(None, None, AXIS), P(None, None, AXIS), P(None, AXIS))
    return jax.shard_map(
        on_device, mesh=mesh, in_specs=placed, out_specs=(P(None, AXIS), P()), check_vma=False
    )
```

```python
import jax
import jax.numpy as jnp
from jax import lax
from jax.experimental import pallas as pl
from jax.experimental.pallas import tpu as pltpu
from jax.sharding import PartitionSpec as P

AXIS = "iface"
LANES = 128
SUBLANES = 8
EPSILON = 1e-06
TOLERANCE = 1e-06
STEPS_PER_TEST = 4
TESTS_MAX = 4
INNER = ('y0', 'z0', 'x1', 'x0', 'c')
STEPS = [('y2', 'y1', 'z2', 'z1')]
ROOT = ('y0', 'z0', 'x1', 'c', 'y2', 'z2')
BITS = ("y2", "y1", "y0", "z2", "z1", "z0", "x1", "x0", "c")


def groups_over(names):
    count = len(BITS)
    root = sum(1 << (count - 1 - BITS.index(name)) for name in names if name in ROOT)
    found = {}
    for device in range(1 << count):
        bits = [((device ^ root) >> (count - 1 - k)) & 1 for k in range(count)]
        key = tuple(b for b, name in zip(bits, BITS) if name not in names)
        found.setdefault(key, []).append(device)
    return [[group[0] ^ root] + [d for d in group if d != group[0] ^ root] for group in map(sorted, found.values())]


def rows_of(x):
    lead = x.shape[:-2]
    fields, n = x.shape[-2:]
    blocks = x.reshape(lead + (fields, n // LANES, LANES))
    return jnp.swapaxes(blocks, -3, -2).reshape(lead + (fields * n // LANES, LANES))


def eye_mask(m):
    return lax.broadcasted_iota(jnp.int32, (m, m), 0) == lax.broadcasted_iota(jnp.int32, (m, m), 1)


def as_row(column, eye):
    return jnp.sum(jnp.where(eye, column, 0.0), axis=0, keepdims=True)


def as_column(row, eye):
    m = eye.shape[0]
    return jnp.broadcast_to(jnp.sum(jnp.where(eye, row, 0.0), axis=1, keepdims=True), (m, m))


def split(x):
    high = x.astype(jnp.bfloat16)
    rest = x - high.astype(jnp.float32)
    middle = rest.astype(jnp.bfloat16)
    return high, middle, (rest - middle.astype(jnp.float32)).astype(jnp.bfloat16)


def gram_kernel(diffs_ref, given_ref, out_ref, staged, residual_ref, products, sems):
    m, rows = diffs_ref.shape[:2]
    tiles = rows // SUBLANES
    first = pltpu.make_async_copy(given_ref, residual_ref, sems.at[tiles])
    first.start()
    copies = [
        pltpu.make_async_copy(
            diffs_ref.at[:, t * SUBLANES : (t + 1) * SUBLANES, :], staged.at[t], sems.at[t]
        )
        for t in range(tiles)
    ]
    for copy in copies:
        copy.start()
    eye = eye_mask(m)
    first.wait()
    residual = residual_ref[...]
    parity = lax.broadcasted_iota(jnp.int32, residual.shape, 0) & 1
    squares = []
    for f in range(2):
        own = jnp.where(parity == f, residual * residual, 0.0)
        total = jnp.sum(jnp.sum(own, axis=0, keepdims=True), axis=1, keepdims=True)
        squares.append(jnp.broadcast_to(total, (1, LANES)))
    projs = [jnp.zeros((m, LANES), jnp.float32)] * 2
    for t in range(tiles):
        copies[t].wait()
        lines = staged.at[t].reshape(m * SUBLANES, LANES)
        for f in range(2):
            parts = []
            for s in range(f, SUBLANES, 2):
                block = lines[pl.ds(s, m, stride=SUBLANES), :]
                row = t * SUBLANES + s
                projs[f] = projs[f] + block * residual_ref[row : row + 1, :]
                parts.append(split(block))
            high, middle, low = (jnp.concatenate(part, axis=1) for part in zip(*parts))
            product = lax.dot_general(
                jnp.concatenate([high, middle, low], axis=0),
                jnp.concatenate([high, middle], axis=0),
                (((1,), (1,)), ((), ())),
                preferred_element_type=jnp.float32,
            )
            products[f] = product if t == 0 else products[f] + product
    grams = []
    for f in range(2):
        product = products[f]
        cross = product[2 * m :, 0:m]
        small = product[m : 2 * m, m:] + (cross + cross.T)
        grams.append(product[0:m, 0:m] + (small + (product[0:m, m:] + product[m : 2 * m, 0:m])))
    below = lax.broadcasted_iota(jnp.int32, (m, m), 0) > lax.broadcasted_iota(jnp.int32, (m, m), 1)
    out_ref[0:m, :] = jnp.where(below, grams[0], grams[1])
    lines = [as_row(jnp.sum(proj, axis=1, keepdims=True), eye) for proj in projs]
    lines += [as_row(grams[0], eye), *squares]
    at = lax.broadcasted_iota(jnp.int32, (out_ref.shape[0] - m, LANES), 0)
    extra = jnp.zeros(at.shape, jnp.float32)
    for i, line in enumerate(lines):
        extra = jnp.where(at == i, line, extra)
    out_ref[m:, :] = extra


def solve_kernel(rows_all, sums_ref, diffs_ref, correction_ref, coefficients_ref, matrix, x, r, p):
    m = diffs_ref.shape[0]
    eye = eye_mask(m)
    below = lax.broadcasted_iota(jnp.int32, (m, m), 0) > lax.broadcasted_iota(jnp.int32, (m, m), 1)
    packed = sums_ref[0:m, :]
    extra = sums_ref[m : m + 8, :]
    w0 = 1.0 / (extra[3:4, :] / rows_all + EPSILON)
    w1 = 1.0 / (extra[4:5, :] / rows_all + EPSILON)
    turned = packed.T
    gram = jnp.where(below, w0 * packed + w1 * turned, w1 * packed + w0 * turned)
    gram = jnp.where(eye, w1 * packed + w0 * extra[2:3, :], gram)
    b_row = -(w0 * extra[0:1, :] + w1 * extra[1:2, :])
    only = jnp.where(eye, gram, 0.0)
    scale_row = lax.rsqrt(jnp.sum(only, axis=0, keepdims=True))
    scale = lax.rsqrt(jnp.broadcast_to(jnp.sum(only, axis=1, keepdims=True), (m, m)))
    matrix[...] = (scale * gram) * scale_row
    b = as_column(b_row * scale_row, eye)
    x[...] = jnp.zeros((m, m), jnp.float32)
    r[...] = b
    p[...] = b

    def dot(u, v):
        return jnp.sum(u * v, axis=0, keepdims=True)

    def ratio(top, bottom):
        return jnp.where(bottom > 0.0, top / jnp.where(bottom > 0.0, bottom, 1.0), 0.0)

    start = dot(b, b)
    limit = start * (TOLERANCE * TOLERANCE)

    def advance(rr):
        held, rest, direction = x[...], r[...], p[...]
        for _ in range(STEPS_PER_TEST):
            rr = dot(rest, rest)
            image = jnp.broadcast_to(
                jnp.sum(matrix[...] * as_row(direction, eye), axis=1, keepdims=True), (m, m)
            )
            alpha = ratio(rr, dot(direction, image))
            after = rr - alpha * (2.0 * dot(rest, image) - alpha * dot(image, image))
            held = held + alpha * direction
            rest = rest - alpha * image
            direction = rest + ratio(jnp.maximum(after, 0.0), rr) * direction
        x[...], r[...], p[...] = held, rest, direction
        rr = dot(rest, rest)
        return (rr - limit)[0, 0], rr

    over, rr = advance(start)
    _, over, _ = lax.while_loop(
        lambda state: (state[0] < TESTS_MAX) & (state[1] > 0.0),
        lambda state: (state[0] + 1, *advance(state[2])),
        (1, over, rr),
    )

    @pl.when(over > 0.0)
    def _():
        r[...] = b

        @pl.loop(0, m)
        def _(k):
            lane = lax.broadcasted_iota(jnp.int32, (m, m), 1)
            line = lax.broadcasted_iota(jnp.int32, (m, m), 0)
            here = matrix[...]
            row = matrix[pl.ds(k, 1), :]
            value = r[pl.ds(k, 1), :]
            column = jnp.sum(jnp.where(lane == k, here, 0.0), axis=1, keepdims=True)
            pivot = jnp.sum(jnp.where(lane[0:1] == k, row, 0.0), axis=1, keepdims=True)
            factor = jnp.where(line == k, 0.0, column / pivot)
            matrix[...] = here - factor * row
            r[...] = r[...] - factor * value

        x[...] = r[...] / jnp.broadcast_to(
            jnp.sum(jnp.where(eye, matrix[...], 0.0), axis=1, keepdims=True), (m, m)
        )

    found = scale * x[...]
    x[...] = found
    coefficients_ref[...] = as_row(found, eye)
    lines = correction_ref.shape[0]
    totals = [jnp.zeros((lines, LANES), jnp.float32) for _ in range(2)]
    for k in range(m):
        totals[k % 2] += diffs_ref[k] * x[k : k + 1, :]
    correction_ref[...] = totals[0] + totals[1]


def local_sums(res_diffs, residual, lines):
    m = res_diffs.shape[0]
    diffs = rows_of(res_diffs)
    rows = diffs.shape[1]
    return pl.pallas_call(
        gram_kernel,
        out_shape=pltpu.VMEM((lines, LANES), jnp.float32),
        in_specs=[pl.BlockSpec(memory_space=pl.ANY), pl.BlockSpec(memory_space=pl.ANY)],
        out_specs=pl.BlockSpec(memory_space=pltpu.VMEM),
        scratch_shapes=[
            pltpu.VMEM((rows // SUBLANES, m, SUBLANES, LANES), jnp.float32),
            pltpu.VMEM((rows, LANES), jnp.float32),
            pltpu.VMEM((2, 3 * m, 2 * m), jnp.float32),
            pltpu.SemaphoreType.DMA((rows // SUBLANES + 1,)),
        ],
        name="gram",
    )(diffs, rows_of(residual))


def solve_and_apply(sums, diffs, rows_all):
    m, lines = diffs.shape[:2]
    square = pltpu.VMEM((m, LANES), jnp.float32)
    correction, coefficients = pl.pallas_call(
        lambda *refs: solve_kernel(rows_all, *refs),
        out_shape=(
            jax.ShapeDtypeStruct((lines, LANES), jnp.float32),
            jax.ShapeDtypeStruct((1, m), jnp.float32),
        ),
        in_specs=[pl.BlockSpec(memory_space=pltpu.VMEM), pl.BlockSpec(memory_space=pltpu.VMEM)],
        out_specs=(pl.BlockSpec(memory_space=pltpu.VMEM), pl.BlockSpec(memory_space=pltpu.VMEM)),
        scratch_shapes=[square, square, square, square],
        name="solve",
    )(pltpu.with_memory_space_constraint(sums, pltpu.VMEM), diffs)
    blocks = correction.reshape(lines // 2, 2, LANES)
    return jnp.swapaxes(blocks, 0, 1).reshape(2, -1), coefficients.reshape(m)


def exchange(chunks, groups):
    return lax.all_to_all(chunks, AXIS, 0, 0, axis_index_groups=groups)


def on_device(res_diffs, out_diffs, residual):
    rows_all = residual.shape[1] * lax.axis_size(AXIS)
    inner = groups_over(INNER)
    pieces = len(inner[0])
    lines = -(-133 // pieces) * pieces
    sums = local_sums(res_diffs, residual, lines)
    sums, out_diffs = lax.optimization_barrier((sums, out_diffs))
    fetched = pltpu.with_memory_space_constraint(rows_of(out_diffs), pltpu.VMEM)
    part = jnp.sum(exchange(sums.reshape(pieces, 1, -1), inner), axis=0)
    for names in STEPS:
        groups = groups_over(names)
        part = jnp.sum(exchange(jnp.broadcast_to(part, (len(groups[0]),) + part.shape), groups), axis=0)
    whole = exchange(jnp.broadcast_to(part, (pieces,) + part.shape), inner)
    return solve_and_apply(whole.reshape(lines, LANES), fetched, rows_all)


def solution(mesh):
    placed = (P(None, None, AXIS), P(None, None, AXIS), P(None, AXIS))
    return jax.shard_map(
        on_device, mesh=mesh, in_specs=placed, out_specs=(P(None, AXIS), P()), check_vma=False
    )
```

```python
import jax
import jax.numpy as jnp
from jax import lax
from jax.experimental import pallas as pl
from jax.experimental.pallas import tpu as pltpu
from jax.sharding import PartitionSpec as P

AXIS = "iface"
LANES = 128
SUBLANES = 8
EPSILON = 1e-06
TOLERANCE = 1e-06
STEPS_PER_TEST = 4
TESTS_MAX = 4
INNER = ('z0', 'x1', 'x0', 'c')
STEPS = [('y2', 'y1', 'y0', 'z2', 'z1')]
ROOT = ('z0', 'x1', 'c', 'y2', 'z2')
BITS = ("y2", "y1", "y0", "z2", "z1", "z0", "x1", "x0", "c")


def groups_over(names):
    count = len(BITS)
    root = sum(1 << (count - 1 - BITS.index(name)) for name in names if name in ROOT)
    found = {}
    for device in range(1 << count):
        bits = [((device ^ root) >> (count - 1 - k)) & 1 for k in range(count)]
        key = tuple(b for b, name in zip(bits, BITS) if name not in names)
        found.setdefault(key, []).append(device)
    return [[group[0] ^ root] + [d for d in group if d != group[0] ^ root][::-1] for group in map(sorted, found.values())]


def rows_of(x):
    lead = x.shape[:-2]
    fields, n = x.shape[-2:]
    blocks = x.reshape(lead + (fields, n // LANES, LANES))
    return jnp.swapaxes(blocks, -3, -2).reshape(lead + (fields * n // LANES, LANES))


def eye_mask(m):
    return lax.broadcasted_iota(jnp.int32, (m, m), 0) == lax.broadcasted_iota(jnp.int32, (m, m), 1)


def as_row(column, eye):
    return jnp.sum(jnp.where(eye, column, 0.0), axis=0, keepdims=True)


def as_column(row, eye):
    m = eye.shape[0]
    return jnp.broadcast_to(jnp.sum(jnp.where(eye, row, 0.0), axis=1, keepdims=True), (m, m))


def split(x):
    high = x.astype(jnp.bfloat16)
    rest = x - high.astype(jnp.float32)
    middle = rest.astype(jnp.bfloat16)
    return high, middle, (rest - middle.astype(jnp.float32)).astype(jnp.bfloat16)


def gram_kernel(diffs_ref, given_ref, out_ref, staged, residual_ref, products, sems):
    m, rows = diffs_ref.shape[:2]
    tiles = rows // SUBLANES
    first = pltpu.make_async_copy(given_ref, residual_ref, sems.at[tiles])
    first.start()
    copies = [
        pltpu.make_async_copy(
            diffs_ref.at[:, t * SUBLANES : (t + 1) * SUBLANES, :], staged.at[t], sems.at[t]
        )
        for t in range(tiles)
    ]
    for copy in copies:
        copy.start()
    eye = eye_mask(m)
    first.wait()
    residual = residual_ref[...]
    parity = lax.broadcasted_iota(jnp.int32, residual.shape, 0) & 1
    squares = []
    for f in range(2):
        own = jnp.where(parity == f, residual * residual, 0.0)
        total = jnp.sum(jnp.sum(own, axis=0, keepdims=True), axis=1, keepdims=True)
        squares.append(jnp.broadcast_to(total, (1, LANES)))
    projs = [jnp.zeros((m, LANES), jnp.float32)] * 2
    for t in range(tiles):
        copies[t].wait()
        lines = staged.at[t].reshape(m * SUBLANES, LANES)
        for f in range(2):
            parts = []
            for s in range(f, SUBLANES, 2):
                block = lines[pl.ds(s, m, stride=SUBLANES), :]
                row = t * SUBLANES + s
                projs[f] = projs[f] + block * residual_ref[row : row + 1, :]
                parts.append(split(block))
            high, middle, low = (jnp.concatenate(part, axis=1) for part in zip(*parts))
            product = lax.dot_general(
                jnp.concatenate([high, middle, low], axis=0),
                jnp.concatenate([high, middle], axis=0),
                (((1,), (1,)), ((), ())),
                preferred_element_type=jnp.float32,
            )
            products[f] = product if t == 0 else products[f] + product
    grams = []
    for f in range(2):
        product = products[f]
        cross = product[2 * m :, 0:m]
        small = product[m : 2 * m, m:] + (cross + cross.T)
        grams.append(product[0:m, 0:m] + (small + (product[0:m, m:] + product[m : 2 * m, 0:m])))
    below = lax.broadcasted_iota(jnp.int32, (m, m), 0) > lax.broadcasted_iota(jnp.int32, (m, m), 1)
    out_ref[0:m, :] = jnp.where(below, grams[0], grams[1])
    lines = [as_row(jnp.sum(proj, axis=1, keepdims=True), eye) for proj in projs]
    lines += [as_row(grams[0], eye), *squares]
    at = lax.broadcasted_iota(jnp.int32, (out_ref.shape[0] - m, LANES), 0)
    extra = jnp.zeros(at.shape, jnp.float32)
    for i, line in enumerate(lines):
        extra = jnp.where(at == i, line, extra)
    out_ref[m:, :] = extra


def solve_kernel(rows_all, sums_ref, diffs_ref, correction_ref, coefficients_ref, matrix, x, r, p):
    m = diffs_ref.shape[0]
    eye = eye_mask(m)
    below = lax.broadcasted_iota(jnp.int32, (m, m), 0) > lax.broadcasted_iota(jnp.int32, (m, m), 1)
    packed = sums_ref[0:m, :]
    extra = sums_ref[m : m + 8, :]
    w0 = 1.0 / (extra[3:4, :] / rows_all + EPSILON)
    w1 = 1.0 / (extra[4:5, :] / rows_all + EPSILON)
    turned = packed.T
    gram = jnp.where(below, w0 * packed + w1 * turned, w1 * packed + w0 * turned)
    gram = jnp.where(eye, w1 * packed + w0 * extra[2:3, :], gram)
    b_row = -(w0 * extra[0:1, :] + w1 * extra[1:2, :])
    only = jnp.where(eye, gram, 0.0)
    scale_row = lax.rsqrt(jnp.sum(only, axis=0, keepdims=True))
    scale = lax.rsqrt(jnp.broadcast_to(jnp.sum(only, axis=1, keepdims=True), (m, m)))
    matrix[...] = (scale * gram) * scale_row
    b = as_column(b_row * scale_row, eye)
    x[...] = jnp.zeros((m, m), jnp.float32)
    r[...] = b
    p[...] = b

    def dot(u, v):
        return jnp.sum(u * v, axis=0, keepdims=True)

    def ratio(top, bottom):
        return jnp.where(bottom > 0.0, top / jnp.where(bottom > 0.0, bottom, 1.0), 0.0)

    start = dot(b, b)
    limit = start * (TOLERANCE * TOLERANCE)

    def advance(rr):
        held, rest, direction = x[...], r[...], p[...]
        for _ in range(STEPS_PER_TEST):
            rr = dot(rest, rest)
            image = jnp.broadcast_to(
                jnp.sum(matrix[...] * as_row(direction, eye), axis=1, keepdims=True), (m, m)
            )
            alpha = ratio(rr, dot(direction, image))
            after = rr - alpha * (2.0 * dot(rest, image) - alpha * dot(image, image))
            held = held + alpha * direction
            rest = rest - alpha * image
            direction = rest + ratio(jnp.maximum(after, 0.0), rr) * direction
        x[...], r[...], p[...] = held, rest, direction
        rr = dot(rest, rest)
        return (rr - limit)[0, 0], rr

    over, rr = advance(start)
    _, over, _ = lax.while_loop(
        lambda state: (state[0] < TESTS_MAX) & (state[1] > 0.0),
        lambda state: (state[0] + 1, *advance(state[2])),
        (1, over, rr),
    )

    @pl.when(over > 0.0)
    def _():
        r[...] = b

        @pl.loop(0, m)
        def _(k):
            lane = lax.broadcasted_iota(jnp.int32, (m, m), 1)
            line = lax.broadcasted_iota(jnp.int32, (m, m), 0)
            here = matrix[...]
            row = matrix[pl.ds(k, 1), :]
            value = r[pl.ds(k, 1), :]
            column = jnp.sum(jnp.where(lane == k, here, 0.0), axis=1, keepdims=True)
            pivot = jnp.sum(jnp.where(lane[0:1] == k, row, 0.0), axis=1, keepdims=True)
            factor = jnp.where(line == k, 0.0, column / pivot)
            matrix[...] = here - factor * row
            r[...] = r[...] - factor * value

        x[...] = r[...] / jnp.broadcast_to(
            jnp.sum(jnp.where(eye, matrix[...], 0.0), axis=1, keepdims=True), (m, m)
        )

    found = scale * x[...]
    x[...] = found
    coefficients_ref[...] = as_row(found, eye)
    lines = correction_ref.shape[0]
    totals = [jnp.zeros((lines, LANES), jnp.float32) for _ in range(2)]
    for k in range(m):
        totals[k % 2] += diffs_ref[k] * x[k : k + 1, :]
    correction_ref[...] = totals[0] + totals[1]


def local_sums(res_diffs, residual, lines):
    m = res_diffs.shape[0]
    diffs = rows_of(res_diffs)
    rows = diffs.shape[1]
    return pl.pallas_call(
        gram_kernel,
        out_shape=pltpu.VMEM((lines, LANES), jnp.float32),
        in_specs=[pl.BlockSpec(memory_space=pl.ANY), pl.BlockSpec(memory_space=pl.ANY)],
        out_specs=pl.BlockSpec(memory_space=pltpu.VMEM),
        scratch_shapes=[
            pltpu.VMEM((rows // SUBLANES, m, SUBLANES, LANES), jnp.float32),
            pltpu.VMEM((rows, LANES), jnp.float32),
            pltpu.VMEM((2, 3 * m, 2 * m), jnp.float32),
            pltpu.SemaphoreType.DMA((rows // SUBLANES + 1,)),
        ],
        name="gram",
    )(diffs, rows_of(residual))


def solve_and_apply(sums, diffs, rows_all):
    m, lines = diffs.shape[:2]
    square = pltpu.VMEM((m, LANES), jnp.float32)
    correction, coefficients = pl.pallas_call(
        lambda *refs: solve_kernel(rows_all, *refs),
        out_shape=(
            jax.ShapeDtypeStruct((lines, LANES), jnp.float32),
            jax.ShapeDtypeStruct((1, m), jnp.float32),
        ),
        in_specs=[pl.BlockSpec(memory_space=pltpu.VMEM), pl.BlockSpec(memory_space=pltpu.VMEM)],
        out_specs=(pl.BlockSpec(memory_space=pltpu.VMEM), pl.BlockSpec(memory_space=pltpu.VMEM)),
        scratch_shapes=[square, square, square, square],
        name="solve",
    )(pltpu.with_memory_space_constraint(sums, pltpu.VMEM), diffs)
    blocks = correction.reshape(lines // 2, 2, LANES)
    return jnp.swapaxes(blocks, 0, 1).reshape(2, -1), coefficients.reshape(m)


def exchange(chunks, groups):
    return lax.all_to_all(chunks, AXIS, 0, 0, axis_index_groups=groups)


def on_device(res_diffs, out_diffs, residual):
    rows_all = residual.shape[1] * lax.axis_size(AXIS)
    inner = groups_over(INNER)
    pieces = len(inner[0])
    lines = -(-133 // pieces) * pieces
    sums = local_sums(res_diffs, residual, lines)
    sums, out_diffs = lax.optimization_barrier((sums, out_diffs))
    fetched = pltpu.with_memory_space_constraint(rows_of(out_diffs), pltpu.VMEM)
    part = jnp.sum(exchange(sums.reshape(pieces, 1, -1), inner), axis=0)
    for names in STEPS:
        groups = groups_over(names)
        part = jnp.sum(exchange(jnp.broadcast_to(part, (len(groups[0]),) + part.shape), groups), axis=0)
    whole = exchange(jnp.broadcast_to(part, (pieces,) + part.shape), inner)
    return solve_and_apply(whole.reshape(lines, LANES), fetched, rows_all)


def solution(mesh):
    placed = (P(None, None, AXIS), P(None, None, AXIS), P(None, AXIS))
    return jax.shard_map(
        on_device, mesh=mesh, in_specs=placed, out_specs=(P(None, AXIS), P()), check_vma=False
    )
```
